32 devices in a mesh: alpha: 4 (over z), beta: 4 (over y, core), task: 2 (over x).
Axes of the slice: x: 2, y: 2, z: 4, core: 2. Of those that a mesh axis runs over, the one named last changes fastest.
Arguments:
- vector: float32 [1024, 4096], P('alpha', 'beta'), may hold values from -6 to 6
- op_alpha: float32 [2, 1024, 1024], P('task', 'alpha'), may hold values from -2 to 2, as said below
- op_beta: float32 [2, 4096, 4096], P('task', 'beta'), may hold values from -2 to 2, as said below
- op_weight: float32 [2], replicated, may hold values from 0.5 to 2
- alpha_string: int32 [1024], P('alpha'), may hold values from 0 to 65535
- beta_string: int32 [4096], P('beta'), may hold values from 0 to 65535
- alpha_energy: float32 [65536], replicated, may hold values from -4 to 4
- beta_energy: float32 [65536], replicated, may hold values from -4 to 4
Outputs:
- sigma: float32 [1024, 4096], P('alpha', ('beta', 'task'))
The draws below stay inside these ranges and needn't reach their ends.
Inputs may be any that keep to these rules, and one draw needn't show every extreme that they name: Every op_alpha[k] is a symmetric matrix. Every op_beta[k] is a symmetric matrix.
All inputs are finite; a program needn't handle non-finite values.
Results may differ from the reference program's by a relative error of at most 0.0001.
Values sent between devices are 32-bit elements; how exact they have to be, the bound alone decides.
A program may use at most 128 MiB of HBM per device.

```python
import math
import jax
import jax.numpy as jnp
from jax import lax

STR = 65536
NA = 1024
NB = 4096
K = 2


def symmetric_stack(key, amount, order):
    raw = jnp.clip(jax.random.normal(key, (amount, order, order), jnp.float32), -4.0, 4.0)
    return (raw + jnp.swapaxes(raw, 1, 2)) * (0.70710678 / jnp.sqrt(jnp.float32(order)))


def draw_op_alpha(key, part):
    return symmetric_stack(jax.random.fold_in(key, 11), K, NA)


def draw_op_beta(key, part):
    return symmetric_stack(jax.random.fold_in(key, 23), K, NB)


def with_ends(drawn, key, smallest, high):
    longest = drawn.shape.index(max(drawn.shape))
    spots = []
    for shift in (0, 1):
        where = [jax.random.randint(jax.random.fold_in(key, axis), (), 0, length) for axis, length in enumerate(drawn.shape)]
        where[longest] = (where[longest] + shift) % drawn.shape[longest]
        spots.append(tuple(where))
    return drawn.at[spots[0]].set(smallest).at[spots[1]].set(high)


def shard_levels(rng, shape, split, low, largest):
    def one(dim, blocks):
        steps = jax.random.uniform(jax.random.fold_in(jax.random.fold_in(rng, 6), dim), (blocks,), jnp.float32, low / len(split), largest / len(split))
        return jnp.repeat(jnp.exp(steps), shape[dim] // blocks).reshape((-1,) + (1,) * (len(shape) - dim - 1))

    gain = one(*split[0])
    for cut in split[1:]:
        gain = gain * one(*cut)
    return gain


def bell_draw(key, extent, scale, most, shards=(), dtype=jnp.bfloat16):
    result = scale * jax.random.normal(key, extent, jnp.float32)
    if shards:
        result = result * shard_levels(key, extent, shards, -0.22, 0.18)
    return jnp.clip(result, -most, most).astype(dtype)


def setup_inputs(seed: int = 0) -> dict:
    arg_keys = jax.random.split(jax.random.key(seed), 9)
    return {
        "vector": bell_draw(arg_keys[0], (NA, NB), 1.0, 6.0, ((0, 4), (1, 4)), jnp.float32),
        "op_alpha": draw_op_alpha(jax.random.fold_in(arg_keys[8], 71), 0),
        "op_beta": draw_op_beta(jax.random.fold_in(arg_keys[8], 71), 0),
        "op_weight": jnp.clip(jnp.exp(jax.random.uniform(arg_keys[3], (K,), jnp.float32, math.log(0.5), math.log(2.0))), 0.5, 2.0),
        "alpha_string": with_ends(jax.random.randint(arg_keys[4], (NA,), 0, STR), jax.random.fold_in(arg_keys[4], 1), 0, STR - 1).astype(jnp.int32),
        "beta_string": with_ends(jax.random.randint(arg_keys[5], (NB,), 0, STR), jax.random.fold_in(arg_keys[5], 1), 0, STR - 1).astype(jnp.int32),
        "alpha_energy": bell_draw(arg_keys[6], (STR,), 1.0, 4.0, (), jnp.float32),
        "beta_energy": bell_draw(arg_keys[7], (STR,), 1.0, 4.0, (), jnp.float32),
    }


def apply_operator(alpha_matrix, beta_matrix, block):
    highest = lax.Precision.HIGHEST
    left_part = jnp.dot(alpha_matrix, block, precision=highest, preferred_element_type=jnp.float32)
    right_part = jnp.dot(block, beta_matrix.T, precision=highest, preferred_element_type=jnp.float32)
    return left_part + right_part


def reference(vector, op_alpha, op_beta, op_weight, alpha_string, beta_string, alpha_energy, beta_energy):
    running = jnp.zeros(vector.shape, jnp.float32)
    for operator in range(K):
        inter = apply_operator(op_alpha[operator], op_beta[operator], vector)
        second = apply_operator(op_alpha[operator], op_beta[operator], inter)
        running = running + op_weight[operator] * second
    diag = alpha_energy[alpha_string][:, None] + beta_energy[beta_string][None, :]
    return diag * vector + 0.5 * running
```

```python
import functools

import jax
import jax.numpy as jnp
from jax import lax
from jax.experimental import pallas as pl
from jax.experimental.pallas import tpu as pltpu
from jax.sharding import PartitionSpec as P

MESH = pl.DeviceIdType.MESH
F32 = jnp.float32
BF16 = jnp.bfloat16
TILE = 256
STRIP = 128
VMEM_BUDGET = 56 * 1024 * 1024


def halves(x):
    high = x.astype(BF16)
    return high, (x - high.astype(F32)).astype(BF16)


def product(stack, right_high, right_low):
    rows = stack.shape[0] // 2
    both = jnp.dot(stack, right_high, preferred_element_type=F32)
    cross = jnp.dot(stack[:rows], right_low, preferred_element_type=F32)
    return both[:rows] + (both[rows:] + cross)


def kernel(
    na, nb, coef_ref, v_ref, a_ref, b_hbm, out_ref,
    strip, bt_high, bt_low, v_all, v_col, a_stack, a_col, square, u_all, total, stack,
    from_task, to_task,
    strip_sem, z_send, z_recv, a_send, a_recv, x_send, x_recv, v_send, v_recv,
    u_send, u_recv, m_send, m_recv, f_send, f_recv,
):
    a = lax.axis_index("alpha")
    b = lax.axis_index("beta")
    t = lax.axis_index("task")
    rows, cols = v_ref.shape
    full_a = a_ref.shape[1]
    half = cols // 2
    parts = half // TILE
    quarter = full_a // nb
    across = lax.rem(b + 2, 4)
    sibling = b + 1 - 2 * lax.rem(b, 2)
    diagonal = lax.rem(sibling + 2, 4)
    other = 1 - t

    barrier = pltpu.get_barrier_semaphore()
    for d in range(1, na):
        pl.semaphore_signal(barrier, inc=1, device_id={"alpha": lax.rem(a + d, na)}, device_id_type=MESH)
    pl.semaphore_signal(barrier, inc=1, device_id={"task": other}, device_id_type=MESH)
    pl.semaphore_signal(barrier, inc=1, device_id={"beta": across}, device_id_type=MESH)
    pl.semaphore_signal(barrier, inc=1, device_id={"beta": sibling}, device_id_type=MESH)
    pl.semaphore_wait(barrier, na + 2)

    def span(start, size):
        return pl.ds(pl.multiple_of(start, 128), size)

    def remote(src, dst, send, recv, where):
        return pltpu.make_async_remote_copy(
            src_ref=src, dst_ref=dst, send_sem=send, recv_sem=recv, device_id=where, device_id_type=MESH
        )

    def piece(side, q):
        return span(side * half + q * TILE, TILE)

    def rows_of(i):
        return pl.ds(pl.multiple_of(i * rows, 8), rows)

    def z_copy(q, d):
        return remote(
            v_ref.at[:, piece(t, q)], v_col.at[rows_of(a), piece(t, q)],
            z_send.at[q, d - 1], z_recv.at[q, d - 1], {"alpha": lax.rem(a + d, na)},
        )

    def x_copy(q, d):
        at = rows_of(lax.rem(a + na - d, na))
        return remote(
            v_col.at[at, piece(t, q)], v_col.at[at, piece(t, q)],
            x_send.at[q, d - 1], x_recv.at[q, d - 1], {"task": other},
        )

    def a_copy(d):
        return remote(
            a_ref.at[:, span(b * quarter, quarter)], a_col.at[rows_of(a), :],
            a_send.at[d - 1], a_recv.at[d - 1], {"alpha": lax.rem(a + d, na)},
        )

    def v_copy(n):
        return (
            lambda: remote(v_ref, v_all.at[b], v_send.at[0], v_recv.at[0], {"beta": across}),
            lambda: remote(v_ref, v_all.at[b], v_send.at[1], v_recv.at[1], {"beta": sibling}),
            lambda: remote(v_all.at[across], v_all.at[across], v_send.at[2], v_recv.at[2], {"beta": sibling}),
        )[n]()

    def u_copy(n, k, side, q):
        block = across if n == 2 else b
        ref = u_all.at[block, :, piece(side, q)]
        where = {"beta": across} if n == 0 else {"beta": sibling}
        return remote(ref, ref, u_send.at[n, k], u_recv.at[n, k], where)

    def m_copy(n):
        ref = square.at[:, span((across if n == 2 else b) * quarter, quarter)]
        where = {"beta": across} if n == 0 else {"beta": sibling}
        return remote(ref, ref, m_send.at[n], m_recv.at[n], where)

    def f_copy(q):
        at = pl.ds(q * TILE, TILE)
        return remote(to_task.at[:, at], from_task.at[:, at], f_send.at[q], f_recv.at[q], {"task": other})

    v_copy(0).start()
    v_copy(1).start()
    for q in range(parts):
        for d in range(1, na):
            z_copy(q, d).start()
    for d in range(1, na):
        a_copy(d).start()

    strips = cols // STRIP

    def strip_copy(r, slot):
        return pltpu.make_async_copy(
            b_hbm.at[pl.ds(pl.multiple_of(r * STRIP, STRIP), STRIP), :], strip.at[slot], strip_sem.at[slot]
        )

    strip_copy(0, 0).start()
    v_col[rows_of(a), :] = v_ref[...]
    a_col[rows_of(a), :] = a_ref[:, span(b * quarter, quarter)]
    a_stack[:rows, :], a_stack[rows:, :] = halves(a_ref[...])

    def take_strip(r, carry):
        slot = lax.rem(r, 2)

        @pl.when(r + 1 < strips)
        def _():
            strip_copy(r + 1, 1 - slot).start()

        strip_copy(r, slot).wait()

        def turn(n, inner):
            at = span(n * 512, 512)
            high, low = halves(strip[slot, :, at].T)
            bt_high[at, span(r * STRIP, STRIP)] = high
            bt_low[at, span(r * STRIP, STRIP)] = low
            return inner

        return lax.fori_loop(0, nb * cols // 512, turn, carry)

    lax.fori_loop(0, strips, take_strip, 0)

    def add_block(value, block, first):
        stack[:rows, :], stack[rows:, :] = halves(value)

        def column(n, carry):
            at = span(n * TILE, TILE)
            depth = span(block * cols, cols)
            term = product(stack[...], bt_high[depth, at], bt_low[depth, at])
            total[:, at] = term if first else total[:, at] + term
            return carry

        lax.fori_loop(0, cols // TILE, column, 0)

    def relay_v(q):
        for d in range(1, na):
            z_copy(q, d).wait_recv()
            x_copy(q, d).start()

    def make_u(k, side, q):
        at = piece(side, q)
        u_all[b, :, at] = total[:, at] + 2.0 * product(a_stack[...], *halves(v_col[:, at]))
        u_copy(0, k, side, q).start()
        u_copy(1, k, side, q).start()

    add_block(v_ref[...], b, True)
    v_copy(1).wait_recv()
    add_block(v_all[sibling], sibling, False)
    relay_v(0)
    v_copy(0).wait_recv()
    v_copy(2).start()
    add_block(v_all[across], across, False)
    v_copy(2).wait_recv()
    add_block(v_all[diagonal], diagonal, False)
    order = []
    for q in range(parts):
        if q > 0:
            relay_v(q)
        make_u(2 * q, t, q)
        for d in range(1, na):
            x_copy(q, d).wait_recv()
        make_u(2 * q + 1, other, q)
        order += [(2 * q, t, q), (2 * q + 1, other, q)]

    add_block(u_all[b], b, True)
    for piece_of in order:
        u_copy(1, *piece_of).wait_recv()
    add_block(u_all[sibling], sibling, False)
    for piece_of in order:
        u_copy(0, *piece_of).wait_recv()
        u_copy(2, *piece_of).start()
    for d in range(1, na):
        a_copy(d).wait_recv()
    square[:, span(b * quarter, quarter)] = product(a_stack[...], *halves(a_col[...]))
    m_copy(0).start()
    m_copy(1).start()
    add_block(u_all[across], across, False)
    for piece_of in order:
        u_copy(2, *piece_of).wait_recv()
    add_block(u_all[diagonal], diagonal, False)
    m_copy(0).wait_recv()
    m_copy(2).start()
    m_copy(1).wait_recv()
    m_copy(2).wait_recv()
    a_stack[:rows, :], a_stack[rows:, :] = halves(square[...])
    coef = coef_ref[0]
    for q in range(parts):
        at = piece(other, q)
        to_task[:, q * TILE:(q + 1) * TILE] = coef * (total[:, at] + product(a_stack[...], *halves(v_col[:, at])))
        f_copy(q).start()
    for q in range(parts):
        at = piece(t, q)
        total[:, at] = coef * (total[:, at] + product(a_stack[...], *halves(v_col[:, at])))
    for q in range(parts):
        f_copy(q).wait_recv()
        out_ref[:, q * TILE:(q + 1) * TILE] = total[:, piece(t, q)] + from_task[:, q * TILE:(q + 1) * TILE]

    for q in range(parts):
        f_copy(q).wait_send()
        for d in range(1, na):
            z_copy(q, d).wait_send()
            x_copy(q, d).wait_send()
    for d in range(1, na):
        a_copy(d).wait_send()
    for n in range(3):
        v_copy(n).wait_send()
        m_copy(n).wait_send()
        for piece_of in order:
            u_copy(n, *piece_of).wait_send()


def scratch(na, nb, rows, cols, full_a):
    quarter = full_a // nb
    parts = cols // 2 // TILE
    buffers = [
        pltpu.VMEM((2, STRIP, nb * cols), F32),
        pltpu.VMEM((nb * cols, cols), BF16),
        pltpu.VMEM((nb * cols, cols), BF16),
        pltpu.VMEM((nb, rows, cols), F32),
        pltpu.VMEM((full_a, cols), F32),
        pltpu.VMEM((2 * rows, full_a), BF16),
        pltpu.VMEM((full_a, quarter), F32),
        pltpu.VMEM((rows, full_a), F32),
        pltpu.VMEM((nb, rows, cols), F32),
        pltpu.VMEM((rows, cols), F32),
        pltpu.VMEM((2 * rows, cols), BF16),
        pltpu.VMEM((rows, cols // 2), F32),
        pltpu.VMEM((rows, cols // 2), F32),
    ]
    dma = pltpu.SemaphoreType.DMA
    counts = [
        (2,), (parts, na - 1), (parts, na - 1), (na - 1,), (na - 1,), (parts, na - 1), (parts, na - 1),
        (3,), (3,), (3, 2 * parts), (3, 2 * parts), (3,), (3,), (parts,), (parts,),
    ]
    return buffers, [dma(c) for c in counts]


def fused(mesh, coefficient, vector, alpha_rows, beta_rows):
    na, nb = mesh.shape["alpha"], mesh.shape["beta"]
    rows, cols = vector.shape
    buffers, semaphores = scratch(na, nb, rows, cols, alpha_rows.shape[1])
    vmem = pl.BlockSpec(memory_space=pltpu.VMEM)
    return pl.pallas_call(
        functools.partial(kernel, na, nb),
        out_shape=jax.ShapeDtypeStruct((rows, cols // 2), F32),
        in_specs=[pl.BlockSpec(memory_space=pltpu.SMEM), vmem, vmem, pl.BlockSpec(memory_space=pl.ANY)],
        out_specs=vmem,
        scratch_shapes=buffers + semaphores,
        compiler_params=pltpu.CompilerParams(
            collective_id=0, has_side_effects=True, vmem_limit_bytes=60 * 1024 * 1024
        ),
    )(coefficient.reshape(1), vector, alpha_rows, beta_rows)


def fits(mesh, vector, alpha_rows):
    na, nb, nt = mesh.shape["alpha"], mesh.shape["beta"], mesh.shape["task"]
    rows, cols = vector.shape
    full_a = alpha_rows.shape[1]
    if nb != 4 or nt != 2 or na < 2 or cols % (2 * TILE) or rows % 8 or full_a % (128 * nb):
        return False
    buffers, _ = scratch(na, nb, rows, cols, full_a)
    size = sum(buf.dtype.itemsize * functools.reduce(lambda x, y: x * y, buf.shape) for buf in buffers)
    size += 4 * (rows * cols + rows * full_a + rows * cols // 2)
    return size < VMEM_BUDGET


def collective(coefficient, vector, alpha_rows, beta_rows):
    high = lax.Precision.HIGH

    def dot(x, y):
        return jnp.dot(x, y, precision=high, preferred_element_type=F32)

    def apply_operator(block):
        left = dot(alpha_rows, lax.all_gather(block, "alpha", axis=0, tiled=True))
        return left + lax.psum_scatter(dot(block, beta_rows), "beta", scatter_dimension=1, tiled=True)

    second = apply_operator(apply_operator(vector))
    return lax.psum_scatter(coefficient * second, "task", scatter_dimension=1, tiled=True)


def on_device(
    mesh, vector, op_alpha, op_beta, op_weight, alpha_string, beta_string, alpha_energy, beta_energy
):
    task_index = lax.axis_index("task")
    coefficient = 0.5 * op_weight[task_index]
    if fits(mesh, vector, op_alpha[0]):
        summed = fused(mesh, coefficient, vector, op_alpha[0], op_beta[0])
    else:
        summed = collective(coefficient, vector, op_alpha[0], op_beta[0])
    width = summed.shape[1]
    column_start = task_index * width
    own_strings = lax.dynamic_slice_in_dim(beta_string, column_start, width, 0)
    own_vector = lax.dynamic_slice_in_dim(vector, column_start, width, 1)
    diag = alpha_energy[alpha_string][:, None] + beta_energy[own_strings][None, :]
    return summed + diag * own_vector


def solution(mesh):
    return jax.shard_map(
        functools.partial(on_device, mesh),
        mesh=mesh,
        in_specs=(
            P("alpha", "beta"),
            P("task", "alpha", None),
            P("task", "beta", None),
            P(),
            P("alpha"),
            P("beta"),
            P(),
            P(),
        ),
        out_specs=P("alpha", ("beta", "task")),
        check_vma=False,
    )
```

```python
import functools

import jax
import jax.numpy as jnp
from jax import lax
from jax.experimental import pallas as pl
from jax.experimental.pallas import tpu as pltpu
from jax.sharding import PartitionSpec as P

MESH = pl.DeviceIdType.MESH
F32 = jnp.float32
BF16 = jnp.bfloat16
TILE = 256
PIECE = 128
STRIP = 128
VMEM_BUDGET = 56 * 1024 * 1024


def halves(x):
    high = x.astype(BF16)
    return high, (x - high.astype(F32)).astype(BF16)


def product(stack, right_high, right_low):
    rows = stack.shape[0] // 2
    both = jnp.dot(stack, right_high, preferred_element_type=F32)
    cross = jnp.dot(stack[:rows], right_low, preferred_element_type=F32)
    return both[:rows] + (both[rows:] + cross)


def look_up(table, index):
    turned = table.T
    high, rest = halves(turned)
    middle = rest
    low = (turned - high.astype(F32) - middle.astype(F32)).astype(BF16)
    shape = (table.shape[0], index.shape[1])
    hot = jnp.where(lax.broadcasted_iota(jnp.int32, shape, 0) == index // 128, 1.0, 0.0).astype(BF16)
    found = jnp.dot(high, hot, preferred_element_type=F32) + (
        jnp.dot(middle, hot, preferred_element_type=F32) + jnp.dot(low, hot, preferred_element_type=F32)
    )
    lane = lax.broadcasted_iota(jnp.int32, found.shape, 0) == lax.rem(index, 128)
    return jnp.sum(jnp.where(lane, found, 0.0), axis=0, keepdims=True)


def kernel(
    na, nb, weight_ref, v_ref, a_ref, alpha_table, beta_table, alpha_index, beta_index, b_hbm, out_ref,
    strip, bt_high, bt_low, v_all, v_col, a_stack, gram, gram_in, scatter, scatter_in,
    square, u_all, total, stack, from_task, to_task, alpha_part, beta_part,
    strip_sem, z_send, z_recv, g_send, g_recv, e_send, e_recv, s_send, s_recv, x_send, x_recv,
    v_send, v_recv, u_send, u_recv, m_send, m_recv, f_send, f_recv,
):
    a = lax.axis_index("alpha")
    b = lax.axis_index("beta")
    t = lax.axis_index("task")
    rows, cols = v_ref.shape
    full_a = a_ref.shape[1]
    half = cols // 2
    parts = half // PIECE
    quarter = full_a // nb
    eighth = quarter // 2
    across = lax.rem(b + 2, 4)
    sibling = b + 1 - 2 * lax.rem(b, 2)
    diagonal = lax.rem(sibling + 2, 4)
    other = 1 - t
    coef = 0.5 * weight_ref[t]

    barrier = pltpu.get_barrier_semaphore()
    for d in range(1, na):
        pl.semaphore_signal(barrier, inc=1, device_id={"alpha": lax.rem(a + d, na)}, device_id_type=MESH)
    pl.semaphore_signal(barrier, inc=1, device_id={"task": other}, device_id_type=MESH)
    pl.semaphore_signal(barrier, inc=1, device_id={"beta": across}, device_id_type=MESH)
    pl.semaphore_signal(barrier, inc=1, device_id={"beta": sibling}, device_id_type=MESH)
    pl.semaphore_wait(barrier, na + 2)

    def span(start, size):
        return pl.ds(pl.multiple_of(start, 128), size)

    def remote(src, dst, send, recv, where):
        return pltpu.make_async_remote_copy(
            src_ref=src, dst_ref=dst, send_sem=send, recv_sem=recv, device_id=where, device_id_type=MESH
        )

    def piece(side, q):
        return span(side * half + q * PIECE, PIECE)

    def rows_of(i):
        return pl.ds(pl.multiple_of(i * rows, 8), rows)

    def z_copy(q, d):
        return remote(
            v_ref.at[:, piece(t, q)], v_col.at[rows_of(a), piece(t, q)],
            z_send.at[q, d - 1], z_recv.at[q, d - 1], {"alpha": lax.rem(a + d, na)},
        )

    def x_copy(q, d):
        at = rows_of(lax.rem(a + na - d, na))
        return remote(
            v_col.at[at, piece(t, q)], v_col.at[at, piece(t, q)],
            x_send.at[q, d - 1], x_recv.at[q, d - 1], {"task": other},
        )

    def g_copy():
        return remote(gram.at[other], gram_in, g_send, g_recv, {"task": other})

    def e_copy(d):
        to = lax.rem(a + d, na)
        return remote(scatter.at[rows_of(to), :], scatter_in.at[d - 1], e_send.at[d - 1], e_recv.at[d - 1], {"alpha": to})

    def s_copy():
        ref = square.at[:, span(b * quarter + t * eighth, eighth)]
        return remote(ref, ref, s_send, s_recv, {"task": other})

    def v_copy(n):
        return (
            lambda: remote(v_ref, v_all.at[b], v_send.at[0], v_recv.at[0], {"beta": across}),
            lambda: remote(v_ref, v_all.at[b], v_send.at[1], v_recv.at[1], {"beta": sibling}),
            lambda: remote(v_all.at[across], v_all.at[across], v_send.at[2], v_recv.at[2], {"beta": sibling}),
        )[n]()

    def u_copy(n, k, side, q):
        block = across if n == 2 else b
        ref = u_all.at[block, :, piece(side, q)]
        where = {"beta": across} if n == 0 else {"beta": sibling}
        return remote(ref, ref, u_send.at[n, k], u_recv.at[n, k], where)

    def m_copy(n):
        ref = square.at[:, span((across if n == 2 else b) * quarter, quarter)]
        where = {"beta": across} if n == 0 else {"beta": sibling}
        return remote(ref, ref, m_send.at[n], m_recv.at[n], where)

    def f_copy(q):
        at = pl.ds(q * TILE, TILE)
        return remote(to_task.at[:, at], from_task.at[:, at], f_send.at[q], f_recv.at[q], {"task": other})

    v_copy(0).start()
    v_copy(1).start()
    for q in range(parts):
        for d in range(1, na):
            z_copy(q, d).start()
    strips = cols // STRIP

    def strip_copy(r, slot):
        return pltpu.make_async_copy(
            b_hbm.at[pl.ds(pl.multiple_of(r * STRIP, STRIP), STRIP), :], strip.at[slot], strip_sem.at[slot]
        )

    strip_copy(0, 0).start()
    v_col[rows_of(a), :] = v_ref[...]
    gram_left, gram_low = halves(a_ref[...].T)
    right_high, right_low = halves(coef * a_ref[:, span(b * quarter, quarter)])
    outer = jnp.dot(gram_left, right_high, preferred_element_type=F32) + (
        jnp.dot(gram_low, right_high, preferred_element_type=F32)
        + jnp.dot(gram_left, right_low, preferred_element_type=F32)
    )
    gram[0] = outer[:, :eighth]
    gram[1] = outer[:, eighth:]
    a_stack[:rows, :], a_stack[rows:, :] = halves(a_ref[...])
    g_copy().start()

    def take_strip(r, carry):
        slot = lax.rem(r, 2)

        @pl.when(r + 1 < strips)
        def _():
            strip_copy(r + 1, 1 - slot).start()

        strip_copy(r, slot).wait()

        def turn(n, inner):
            at = span(n * 512, 512)
            high, low = halves(strip[slot, :, at].T)
            bt_high[at, span(r * STRIP, STRIP)] = high
            bt_low[at, span(r * STRIP, STRIP)] = low
            return inner

        return lax.fori_loop(0, nb * cols // 512, turn, carry)

    lax.fori_loop(0, strips, take_strip, 0)

    def load_block(value):
        stack[:rows, :], stack[rows:, :] = halves(value)

    def add_columns(block, first, start, size):
        def column(n, carry):
            at = span(start + n * TILE, TILE)
            depth = span(block * cols, cols)
            term = product(stack[...], bt_high[depth, at], bt_low[depth, at])
            total[:, at] = term if first else total[:, at] + term
            return carry

        lax.fori_loop(0, size // TILE, column, 0)

    def add_block(value, block, first):
        load_block(value)
        add_columns(block, first, 0, cols)

    def relay_v(q):
        for d in range(1, na):
            z_copy(q, d).wait_recv()
            x_copy(q, d).start()

    def make_u(k, side, q):
        at = piece(side, q)
        u_all[b, :, at] = total[:, at] + 2.0 * product(a_stack[...], *halves(v_col[:, at]))
        u_copy(0, k, side, q).start()
        u_copy(1, k, side, q).start()

    add_block(v_ref[...], b, True)
    g_copy().wait_recv()
    scatter[...] = gram[t] + gram_in[...]
    relay_v(0)
    for d in range(1, na):
        e_copy(d).start()
    v_copy(1).wait_recv()
    add_block(v_all[sibling], sibling, False)
    beta_part[...] = look_up(beta_table[...], beta_index[:, span(t * half, half)])
    alpha_row = look_up(alpha_table[...], alpha_index[...])
    alpha_part[...] = jnp.broadcast_to(alpha_row, (128, rows)).T
    relay_v(1)
    v_copy(0).wait_recv()
    v_copy(2).start()
    add_block(v_all[across], across, False)
    v_copy(2).wait_recv()
    add_block(v_all[diagonal], diagonal, False)

    order = []

    def make_next(side, q):
        make_u(len(order), side, q)
        order.append((len(order), side, q))

    for q in range(parts + 1):
        if 2 <= q < parts:
            relay_v(q)
        if q < parts:
            make_next(t, q)
        if q > 0:
            for d in range(1, na):
                x_copy(q - 1, d).wait_recv()
            make_next(other, q - 1)

    def relay_u(pieces):
        for piece_of in pieces:
            u_copy(0, *piece_of).wait_recv()
            u_copy(2, *piece_of).start()

    relay_u(order[:-2])
    add_block(u_all[b], b, True)
    for d in range(1, na):
        e_copy(d).wait_recv()
    mine = scatter[rows_of(a), :]
    for d in range(1, na):
        mine = mine + scatter_in[d - 1]
    square[:, span(b * quarter + t * eighth, eighth)] = mine
    for piece_of in order:
        u_copy(1, *piece_of).wait_recv()
    s_copy().start()
    relay_u(order[-2:])
    add_block(u_all[sibling], sibling, False)
    s_copy().wait_recv()
    m_copy(0).start()
    m_copy(1).start()
    add_block(u_all[across], across, False)
    for piece_of in order:
        u_copy(2, *piece_of).wait_recv()
    load_block(u_all[diagonal])
    for q in range(half // TILE):
        at = span(other * half + q * TILE, TILE)
        add_columns(diagonal, False, other * half + q * TILE, TILE)
        to_task[:, q * TILE:(q + 1) * TILE] = coef * total[:, at]
        f_copy(q).start()
    add_columns(diagonal, False, t * half, half)
    m_copy(0).wait_recv()
    m_copy(2).start()
    m_copy(1).wait_recv()
    m_copy(2).wait_recv()
    a_stack[:rows, :], a_stack[rows:, :] = halves(square[...])
    for q in range(half // TILE):
        at = span(t * half + q * TILE, TILE)
        local = pl.ds(q * TILE, TILE)
        diag = alpha_part[:, :1] + beta_part[:, local]
        total[:, at] = (
            coef * total[:, at] + product(a_stack[...], *halves(v_col[:, at])) + diag * v_ref[:, at]
        )
    for q in range(half // TILE):
        f_copy(q).wait_recv()
        local = pl.ds(q * TILE, TILE)
        out_ref[:, local] = total[:, span(t * half + q * TILE, TILE)] + from_task[:, local]

    for q in range(half // TILE):
        f_copy(q).wait_send()
    for q in range(parts):
        for d in range(1, na):
            z_copy(q, d).wait_send()
            x_copy(q, d).wait_send()
    g_copy().wait_send()
    s_copy().wait_send()
    for d in range(1, na):
        e_copy(d).wait_send()
    for n in range(3):
        v_copy(n).wait_send()
        m_copy(n).wait_send()
        for piece_of in order:
            u_copy(n, *piece_of).wait_send()


def scratch(na, nb, rows, cols, full_a):
    quarter = full_a // nb
    eighth = quarter // 2
    parts = cols // 2 // PIECE
    buffers = [
        pltpu.VMEM((2, STRIP, nb * cols), F32),
        pltpu.VMEM((nb * cols, cols), BF16),
        pltpu.VMEM((nb * cols, cols), BF16),
        pltpu.VMEM((nb, rows, cols), F32),
        pltpu.VMEM((full_a, cols), F32),
        pltpu.VMEM((2 * rows, full_a), BF16),
        pltpu.VMEM((2, full_a, eighth), F32),
        pltpu.VMEM((full_a, eighth), F32),
        pltpu.VMEM((full_a, eighth), F32),
        pltpu.VMEM((na - 1, rows, eighth), F32),
        pltpu.VMEM((rows, full_a), F32),
        pltpu.VMEM((nb, rows, cols), F32),
        pltpu.VMEM((rows, cols), F32),
        pltpu.VMEM((2 * rows, cols), BF16),
        pltpu.VMEM((rows, cols // 2), F32),
        pltpu.VMEM((rows, cols // 2), F32),
        pltpu.VMEM((rows, 128), F32),
        pltpu.VMEM((1, cols // 2), F32),
    ]
    dma = pltpu.SemaphoreType.DMA
    tiles = cols // 2 // TILE
    counts = [
        (2,), (parts, na - 1), (parts, na - 1), (), (), (na - 1,), (na - 1,), (), (), (parts, na - 1), (parts, na - 1),
        (3,), (3,), (3, 2 * parts), (3, 2 * parts), (3,), (3,), (tiles,), (tiles,),
    ]
    return buffers, [dma(c) if c else dma for c in counts]


def fused(
    mesh, op_weight, vector, alpha_rows, beta_rows, alpha_string, beta_string, alpha_energy, beta_energy
):
    na, nb = mesh.shape["alpha"], mesh.shape["beta"]
    rows, cols = vector.shape
    buffers, semaphores = scratch(na, nb, rows, cols, alpha_rows.shape[1])
    vmem = pl.BlockSpec(memory_space=pltpu.VMEM)
    return pl.pallas_call(
        functools.partial(kernel, na, nb),
        out_shape=jax.ShapeDtypeStruct((rows, cols // 2), F32),
        in_specs=[pl.BlockSpec(memory_space=pltpu.SMEM)] + [vmem] * 6 + [pl.BlockSpec(memory_space=pl.ANY)],
        out_specs=vmem,
        scratch_shapes=buffers + semaphores,
        compiler_params=pltpu.CompilerParams(
            collective_id=0, has_side_effects=True, vmem_limit_bytes=60 * 1024 * 1024
        ),
    )(
        op_weight, vector, alpha_rows, alpha_energy.reshape(-1, 128), beta_energy.reshape(-1, 128),
        alpha_string.reshape(1, -1), beta_string.reshape(1, -1), beta_rows,
    )


def fits(mesh, vector, alpha_rows, alpha_energy, beta_energy):
    na, nb, nt = mesh.shape["alpha"], mesh.shape["beta"], mesh.shape["task"]
    rows, cols = vector.shape
    full_a = alpha_rows.shape[1]
    if nb != 4 or nt != 2 or na < 2 or cols % (2 * TILE) or rows % 128 or full_a % (256 * nb):
        return False
    if cols // 2 < 2 * PIECE or alpha_energy.size % 128 or beta_energy.size % 128:
        return False
    buffers, _ = scratch(na, nb, rows, cols, full_a)
    size = sum(buf.dtype.itemsize * functools.reduce(lambda x, y: x * y, buf.shape) for buf in buffers)
    size += 4 * (rows * cols + rows * full_a + rows * cols // 2)
    return size < VMEM_BUDGET


def collective(coefficient, vector, alpha_rows, beta_rows):
    high = lax.Precision.HIGH

    def dot(x, y):
        return jnp.dot(x, y, precision=high, preferred_element_type=F32)

    def apply_operator(block):
        left = dot(alpha_rows, lax.all_gather(block, "alpha", axis=0, tiled=True))
        return left + lax.psum_scatter(dot(block, beta_rows), "beta", scatter_dimension=1, tiled=True)

    second = apply_operator(apply_operator(vector))
    return lax.psum_scatter(coefficient * second, "task", scatter_dimension=1, tiled=True)


def on_device(
    mesh, vector, op_alpha, op_beta, op_weight, alpha_string, beta_string, alpha_energy, beta_energy
):
    if fits(mesh, vector, op_alpha[0], alpha_energy, beta_energy):
        return fused(
            mesh, op_weight, vector, op_alpha[0], op_beta[0],
            alpha_string, beta_string, alpha_energy, beta_energy,
        )
    task_index = lax.axis_index("task")
    summed = collective(0.5 * op_weight[task_index], vector, op_alpha[0], op_beta[0])
    width = summed.shape[1]
    column_start = task_index * width
    own_strings = lax.dynamic_slice_in_dim(beta_string, column_start, width, 0)
    own_vector = lax.dynamic_slice_in_dim(vector, column_start, width, 1)
    diag = alpha_energy[alpha_string][:, None] + beta_energy[own_strings][None, :]
    return summed + diag * own_vector


def solution(mesh):
    return jax.shard_map(
        functools.partial(on_device, mesh),
        mesh=mesh,
        in_specs=(
            P("alpha", "beta"),
            P("task", "alpha", None),
            P("task", "beta", None),
            P(),
            P("alpha"),
            P("beta"),
            P(),
            P(),
        ),
        out_specs=P("alpha", ("beta", "task")),
        check_vma=False,
    )
```

```python
import functools

import jax
import jax.numpy as jnp
from jax import lax
from jax.experimental import pallas as pl
from jax.experimental.pallas import tpu as pltpu
from jax.sharding import PartitionSpec as P

MESH = pl.DeviceIdType.MESH
F32 = jnp.float32
BF16 = jnp.bfloat16
TILE = 256
PIECE = 128
STRIP = 128
VMEM_BUDGET = 56 * 1024 * 1024


def halves(x):
    high = x.astype(BF16)
    return high, (x - high.astype(F32)).astype(BF16)


def product(stack, right_high, right_low):
    rows = stack.shape[0] // 2
    both = jnp.dot(stack, right_high, preferred_element_type=F32)
    cross = jnp.dot(stack[:rows], right_low, preferred_element_type=F32)
    return both[:rows] + (both[rows:] + cross)


def look_up(table, index):
    turned = table.T
    high, rest = halves(turned)
    middle = rest
    low = (turned - high.astype(F32) - middle.astype(F32)).astype(BF16)
    shape = (table.shape[0], index.shape[1])
    hot = jnp.where(lax.broadcasted_iota(jnp.int32, shape, 0) == index // 128, 1.0, 0.0).astype(BF16)
    found = jnp.dot(high, hot, preferred_element_type=F32) + (
        jnp.dot(middle, hot, preferred_element_type=F32) + jnp.dot(low, hot, preferred_element_type=F32)
    )
    lane = lax.broadcasted_iota(jnp.int32, found.shape, 0) == lax.rem(index, 128)
    return jnp.sum(jnp.where(lane, found, 0.0), axis=0, keepdims=True)


def kernel(
    na, nb, weight_ref, v_ref, a_ref, alpha_table, beta_table, alpha_index, beta_index, b_hbm, out_ref,
    strip, bt_high, bt_low, v_all, v_col, a_stack, gram, gram_in, scatter, scatter_in,
    square, u_all, total, stack, from_task, to_task, alpha_part, beta_part,
    strip_sem, z_send, z_recv, r_send, g_send, g_recv, e_send, e_recv, s_send, s_recv, x_send, x_recv,
    v_send, v_recv, u_send, u_recv, m_send, m_recv, f_send, f_recv,
):
    a = lax.axis_index("alpha")
    b = lax.axis_index("beta")
    t = lax.axis_index("task")
    rows, cols = v_ref.shape
    full_a = a_ref.shape[1]
    half = cols // 2
    parts = half // PIECE
    quarter = full_a // nb
    eighth = quarter // 2
    across = lax.rem(b + 2, 4)
    sibling = b + 1 - 2 * lax.rem(b, 2)
    diagonal = lax.rem(sibling + 2, 4)
    other = 1 - t
    coef = 0.5 * weight_ref[t]
    inner = lax.rem(a + 1, 4) >= 2

    def peer(d):
        return (a, a + 1 - 2 * lax.rem(a, 2), lax.rem(a + 2, 4), 3 - a)[d]

    barrier = pltpu.get_barrier_semaphore()
    for d in range(1, na):
        pl.semaphore_signal(barrier, inc=1, device_id={"alpha": lax.rem(a + d, na)}, device_id_type=MESH)
    pl.semaphore_signal(barrier, inc=1, device_id={"task": other}, device_id_type=MESH)
    pl.semaphore_signal(barrier, inc=1, device_id={"beta": across}, device_id_type=MESH)
    pl.semaphore_signal(barrier, inc=1, device_id={"beta": sibling}, device_id_type=MESH)
    pl.semaphore_wait(barrier, na + 2)

    def span(start, size):
        return pl.ds(pl.multiple_of(start, 128), size)

    def remote(src, dst, send, recv, where):
        return pltpu.make_async_remote_copy(
            src_ref=src, dst_ref=dst, send_sem=send, recv_sem=recv, device_id=where, device_id_type=MESH
        )

    def piece(side, q):
        return span(side * half + q * PIECE, PIECE)

    def rows_of(i):
        return pl.ds(pl.multiple_of(i * rows, 8), rows)

    def z_copy(q, d):
        return remote(
            v_ref.at[:, piece(t, q)], v_col.at[rows_of(a), piece(t, q)],
            z_send.at[q, d - 1], z_recv.at[q, d - 1], {"alpha": peer(d)},
        )

    def z_relay(q):
        ref = v_col.at[rows_of(peer(2)), piece(t, q)]
        return remote(ref, ref, r_send.at[q], z_recv.at[q, 2], {"alpha": peer(1)})

    def x_copy(q, d):
        at = rows_of(peer(d))
        return remote(
            v_col.at[at, piece(t, q)], v_col.at[at, piece(t, q)],
            x_send.at[q, d - 1], x_recv.at[q, d - 1], {"task": other},
        )

    def g_copy():
        return remote(gram.at[other], gram_in, g_send, g_recv, {"task": other})

    def e_copy(d):
        to = peer(d)
        return remote(scatter.at[rows_of(to), :], scatter_in.at[d - 1], e_send.at[d - 1], e_recv.at[d - 1], {"alpha": to})

    def s_copy():
        ref = square.at[:, span(b * quarter + t * eighth, eighth)]
        return remote(ref, ref, s_send, s_recv, {"task": other})

    def v_copy(n):
        return (
            lambda: remote(v_ref, v_all.at[b], v_send.at[0], v_recv.at[0], {"beta": across}),
            lambda: remote(v_ref, v_all.at[b], v_send.at[1], v_recv.at[1], {"beta": sibling}),
            lambda: remote(v_all.at[across], v_all.at[across], v_send.at[2], v_recv.at[2], {"beta": sibling}),
        )[n]()

    def u_copy(n, k, side, q):
        block = across if n == 2 else b
        ref = u_all.at[block, :, piece(side, q)]
        where = {"beta": across} if n == 0 else {"beta": sibling}
        return remote(ref, ref, u_send.at[n, k], u_recv.at[n, k], where)

    def m_copy(n):
        ref = square.at[:, span((across if n == 2 else b) * quarter, quarter)]
        where = {"beta": across} if n == 0 else {"beta": sibling}
        return remote(ref, ref, m_send.at[n], m_recv.at[n], where)

    def f_copy(q):
        at = pl.ds(q * TILE, TILE)
        return remote(to_task.at[:, at], from_task.at[:, at], f_send.at[q], f_recv.at[q], {"task": other})

    v_copy(0).start()
    v_copy(1).start()
    for q in range(parts):
        z_copy(q, 1).start()
        z_copy(q, 2).start()

        @pl.when(inner)
        def _():
            z_copy(q, 3).start()
    strips = cols // STRIP

    def strip_copy(r, slot):
        return pltpu.make_async_copy(
            b_hbm.at[pl.ds(pl.multiple_of(r * STRIP, STRIP), STRIP), :], strip.at[slot], strip_sem.at[slot]
        )

    strip_copy(0, 0).start()
    v_col[rows_of(a), :] = v_ref[...]
    gram_left, gram_low = halves(a_ref[...].T)
    right_high, right_low = halves(coef * a_ref[:, span(b * quarter, quarter)])
    outer = jnp.dot(gram_left, right_high, preferred_element_type=F32) + (
        jnp.dot(gram_low, right_high, preferred_element_type=F32)
        + jnp.dot(gram_left, right_low, preferred_element_type=F32)
    )
    gram[0] = outer[:, :eighth]
    gram[1] = outer[:, eighth:]
    a_stack[:rows, :], a_stack[rows:, :] = halves(a_ref[...])
    g_copy().start()

    def take_strip(r, carry):
        slot = lax.rem(r, 2)

        @pl.when(r + 1 < strips)
        def _():
            strip_copy(r + 1, 1 - slot).start()

        strip_copy(r, slot).wait()

        def turn(n, inner):
            at = span(n * 512, 512)
            high, low = halves(strip[slot, :, at].T)
            bt_high[at, span(r * STRIP, STRIP)] = high
            bt_low[at, span(r * STRIP, STRIP)] = low
            return inner

        return lax.fori_loop(0, nb * cols // 512, turn, carry)

    lax.fori_loop(0, strips, take_strip, 0)

    def load_block(value):
        stack[:rows, :], stack[rows:, :] = halves(value)

    def add_columns(block, first, start, size):
        def column(n, carry):
            at = span(start + n * TILE, TILE)
            depth = span(block * cols, cols)
            term = product(stack[...], bt_high[depth, at], bt_low[depth, at])
            total[:, at] = term if first else total[:, at] + term
            return carry

        lax.fori_loop(0, size // TILE, column, 0)

    def add_block(value, block, first):
        load_block(value)
        add_columns(block, first, 0, cols)

    def relay_v(q):
        z_copy(q, 2).wait_recv()

        @pl.when(inner)
        def _():
            z_relay(q).start()

        x_copy(q, 2).start()
        for d in (1, 3):
            z_copy(q, d).wait_recv()
            x_copy(q, d).start()

    def make_u(k, side, q):
        at = piece(side, q)
        u_all[b, :, at] = total[:, at] + 2.0 * product(a_stack[...], *halves(v_col[:, at]))
        u_copy(0, k, side, q).start()
        u_copy(1, k, side, q).start()

    add_block(v_ref[...], b, True)
    g_copy().wait_recv()
    scatter[...] = gram[t] + gram_in[...]
    relay_v(0)
    for d in range(1, na):
        e_copy(d).start()
    v_copy(1).wait_recv()
    add_block(v_all[sibling], sibling, False)
    beta_part[...] = look_up(beta_table[...], beta_index[:, span(t * half, half)])
    alpha_row = look_up(alpha_table[...], alpha_index[...])
    alpha_part[...] = jnp.broadcast_to(alpha_row, (128, rows)).T
    relay_v(1)
    v_copy(0).wait_recv()
    v_copy(2).start()
    add_block(v_all[across], across, False)
    v_copy(2).wait_recv()
    add_block(v_all[diagonal], diagonal, False)

    order = []

    def make_next(side, q):
        make_u(len(order), side, q)
        order.append((len(order), side, q))

    for q in range(parts + 1):
        if 2 <= q < parts:
            relay_v(q)
        if q < parts:
            make_next(t, q)
        if q > 0:
            for d in range(1, na):
                x_copy(q - 1, d).wait_recv()
            make_next(other, q - 1)

    def relay_u(pieces):
        for piece_of in pieces:
            u_copy(0, *piece_of).wait_recv()
            u_copy(2, *piece_of).start()

    relay_u(order[:-2])
    add_block(u_all[b], b, True)
    for d in range(1, na):
        e_copy(d).wait_recv()
    mine = scatter[rows_of(a), :]
    for d in range(1, na):
        mine = mine + scatter_in[d - 1]
    square[:, span(b * quarter + t * eighth, eighth)] = mine
    for piece_of in order:
        u_copy(1, *piece_of).wait_recv()
    s_copy().start()
    relay_u(order[-2:])
    load_block(u_all[sibling])
    add_columns(sibling, False, other * half, half)
    s_copy().wait_recv()
    m_copy(0).start()
    m_copy(1).start()
    load_block(u_all[across])
    add_columns(across, False, other * half, half)
    for piece_of in order:
        u_copy(2, *piece_of).wait_recv()
    load_block(u_all[diagonal])
    for q in range(half // TILE):
        at = span(other * half + q * TILE, TILE)
        add_columns(diagonal, False, other * half + q * TILE, TILE)
        to_task[:, q * TILE:(q + 1) * TILE] = coef * total[:, at]
        f_copy(q).start()

    def own_half(n, carry):
        block = lax.rem(b + n, nb)
        load_block(u_all[block])
        add_columns(block, False, t * half, half)
        return carry

    lax.fori_loop(1, nb, own_half, 0)
    m_copy(0).wait_recv()
    m_copy(2).start()
    m_copy(1).wait_recv()
    m_copy(2).wait_recv()
    a_stack[:rows, :], a_stack[rows:, :] = halves(square[...])
    for q in range(half // TILE):
        at = span(t * half + q * TILE, TILE)
        local = pl.ds(q * TILE, TILE)
        diag = alpha_part[:, :1] + beta_part[:, local]
        total[:, at] = (
            coef * total[:, at] + product(a_stack[...], *halves(v_col[:, at])) + diag * v_ref[:, at]
        )
    for q in range(half // TILE):
        f_copy(q).wait_recv()
        local = pl.ds(q * TILE, TILE)
        out_ref[:, local] = total[:, span(t * half + q * TILE, TILE)] + from_task[:, local]

    for q in range(half // TILE):
        f_copy(q).wait_send()
    for q in range(parts):
        z_copy(q, 1).wait_send()
        z_copy(q, 2).wait_send()

        @pl.when(inner)
        def _():
            z_copy(q, 3).wait_send()
            z_relay(q).wait_send()

        for d in range(1, na):
            x_copy(q, d).wait_send()
    g_copy().wait_send()
    s_copy().wait_send()
    for d in range(1, na):
        e_copy(d).wait_send()
    for n in range(3):
        v_copy(n).wait_send()
        m_copy(n).wait_send()
        for piece_of in order:
            u_copy(n, *piece_of).wait_send()


def scratch(na, nb, rows, cols, full_a):
    quarter = full_a // nb
    eighth = quarter // 2
    parts = cols // 2 // PIECE
    buffers = [
        pltpu.VMEM((2, STRIP, nb * cols), F32),
        pltpu.VMEM((nb * cols, cols), BF16),
        pltpu.VMEM((nb * cols, cols), BF16),
        pltpu.VMEM((nb, rows, cols), F32),
        pltpu.VMEM((full_a, cols), F32),
        pltpu.VMEM((2 * rows, full_a), BF16),
        pltpu.VMEM((2, full_a, eighth), F32),
        pltpu.VMEM((full_a, eighth), F32),
        pltpu.VMEM((full_a, eighth), F32),
        pltpu.VMEM((na - 1, rows, eighth), F32),
        pltpu.VMEM((rows, full_a), F32),
        pltpu.VMEM((nb, rows, cols), F32),
        pltpu.VMEM((rows, cols), F32),
        pltpu.VMEM((2 * rows, cols), BF16),
        pltpu.VMEM((rows, cols // 2), F32),
        pltpu.VMEM((rows, cols // 2), F32),
        pltpu.VMEM((rows, 128), F32),
        pltpu.VMEM((1, cols // 2), F32),
    ]
    dma = pltpu.SemaphoreType.DMA
    tiles = cols // 2 // TILE
    counts = [
        (2,), (parts, na - 1), (parts, na - 1), (parts,), (), (), (na - 1,), (na - 1,), (), (), (parts, na - 1), (parts, na - 1),
        (3,), (3,), (3, 2 * parts), (3, 2 * parts), (3,), (3,), (tiles,), (tiles,),
    ]
    return buffers, [dma(c) if c else dma for c in counts]


def fused(
    mesh, op_weight, vector, alpha_rows, beta_rows, alpha_string, beta_string, alpha_energy, beta_energy
):
    na, nb = mesh.shape["alpha"], mesh.shape["beta"]
    rows, cols = vector.shape
    buffers, semaphores = scratch(na, nb, rows, cols, alpha_rows.shape[1])
    vmem = pl.BlockSpec(memory_space=pltpu.VMEM)
    return pl.pallas_call(
        functools.partial(kernel, na, nb),
        out_shape=jax.ShapeDtypeStruct((rows, cols // 2), F32),
        in_specs=[pl.BlockSpec(memory_space=pltpu.SMEM)] + [vmem] * 6 + [pl.BlockSpec(memory_space=pl.ANY)],
        out_specs=vmem,
        scratch_shapes=buffers + semaphores,
        compiler_params=pltpu.CompilerParams(
            collective_id=0, has_side_effects=True, vmem_limit_bytes=60 * 1024 * 1024
        ),
    )(
        op_weight, vector, alpha_rows, alpha_energy.reshape(-1, 128), beta_energy.reshape(-1, 128),
        alpha_string.reshape(1, -1), beta_string.reshape(1, -1), beta_rows,
    )


def fits(mesh, vector, alpha_rows, alpha_energy, beta_energy):
    na, nb, nt = mesh.shape["alpha"], mesh.shape["beta"], mesh.shape["task"]
    rows, cols = vector.shape
    full_a = alpha_rows.shape[1]
    if nb != 4 or nt != 2 or na != 4 or cols % (2 * TILE) or rows % 128 or full_a % (256 * nb):
        return False
    if cols // 2 < 2 * PIECE or alpha_energy.size % 128 or beta_energy.size % 128:
        return False
    buffers, _ = scratch(na, nb, rows, cols, full_a)
    size = sum(buf.dtype.itemsize * functools.reduce(lambda x, y: x * y, buf.shape) for buf in buffers)
    size += 4 * (rows * cols + rows * full_a + rows * cols // 2)
    return size < VMEM_BUDGET


def collective(coefficient, vector, alpha_rows, beta_rows):
    high = lax.Precision.HIGH

    def dot(x, y):
        return jnp.dot(x, y, precision=high, preferred_element_type=F32)

    def apply_operator(block):
        left = dot(alpha_rows, lax.all_gather(block, "alpha", axis=0, tiled=True))
        return left + lax.psum_scatter(dot(block, beta_rows), "beta", scatter_dimension=1, tiled=True)

    second = apply_operator(apply_operator(vector))
    return lax.psum_scatter(coefficient * second, "task", scatter_dimension=1, tiled=True)


def on_device(
    mesh, vector, op_alpha, op_beta, op_weight, alpha_string, beta_string, alpha_energy, beta_energy
):
    if fits(mesh, vector, op_alpha[0], alpha_energy, beta_energy):
        return fused(
            mesh, op_weight, vector, op_alpha[0], op_beta[0],
            alpha_string, beta_string, alpha_energy, beta_energy,
        )
    task_index = lax.axis_index("task")
    summed = collective(0.5 * op_weight[task_index], vector, op_alpha[0], op_beta[0])
    width = summed.shape[1]
    column_start = task_index * width
    own_strings = lax.dynamic_slice_in_dim(beta_string, column_start, width, 0)
    own_vector = lax.dynamic_slice_in_dim(vector, column_start, width, 1)
    diag = alpha_energy[alpha_string][:, None] + beta_energy[own_strings][None, :]
    return summed + diag * own_vector


def solution(mesh):
    return jax.shard_map(
        functools.partial(on_device, mesh),
        mesh=mesh,
        in_specs=(
            P("alpha", "beta"),
            P("task", "alpha", None),
            P("task", "beta", None),
            P(),
            P("alpha"),
            P("beta"),
            P(),
            P(),
        ),
        out_specs=P("alpha", ("beta", "task")),
        check_vma=False,
    )
```
